256 devices in a mesh: kring: 16 (over y_lo, x, core), cuts: 16 (over z, y_hi).
Axes of the slice: x: 4, y: 4 (y_hi: 2, y_lo: 2; y = y_hi * 2 + y_lo), z: 8, core: 2. Of those that a mesh axis runs over, the one named last changes fastest.
Arguments:
- blocks: bfloat16 [16, 768, 4096], P('kring', None, 'cuts'), may hold values from -0.75 to 0.75
- vir_energy: bfloat16 [16, 768], P('kring'), may hold values from 0.29882812 to 3
- occ_energy: bfloat16 [16], P('kring'), may hold values from -1 to -0.19921875
- partner: int32 [1, 16], replicated, may hold values from 0 to 15, each once within a row
Outputs:
- gamma_own: bfloat16 [16, 768, 4096], P('kring', None, 'cuts')
- gamma_partner: bfloat16 [1, 16, 768, 4096], P(None, 'kring', None, 'cuts')
The draws below stay inside these ranges and needn't reach their ends.
Inputs may be any that keep to these rules, and one draw needn't show every extreme that they name: Each row of partner names every k-point exactly once.
All inputs are finite; a program needn't handle non-finite values.
Results may differ from the reference program's by a relative error of at most 0.0055.
Values may be sent and summed in bfloat16 or wider, within the bound.
A program may use at most 64 MiB of HBM per device.

```python
import jax
import jax.numpy as jnp
from jax import lax

VIRT = 768
NAUX = 4096
NQ = 1
NK = 16


def raised(entries, key, source, target, shards_of, factor):
    def block_of(axis_at):
        return (jnp.arange(entries.shape[axis_at]) // (entries.shape[axis_at] // shards_of)).reshape((-1,) + (1,) * (entries.ndim - 1 - axis_at))

    near = jax.random.permutation(key, shards_of)[block_of(target)]
    second = (block_of(target) + shards_of // 2) % shards_of
    return jnp.where((block_of(source) == near) | (block_of(source) == second), factor * entries, entries)


def shard_levels(key, extent, shards, low, high):
    factor_of = 1.0
    for dim, blocks in shards:
        draws = jax.random.uniform(jax.random.fold_in(jax.random.fold_in(key, 6), dim), (blocks,), jnp.float32, low / len(shards), high / len(shards))
        factor_of = factor_of * jnp.repeat(jnp.exp(draws), extent[dim] // blocks).reshape((-1,) + (1,) * (len(extent) - 1 - dim))
    return factor_of


def noise_with(stream_key, extent, scale, reach, split, heavy, kind=jnp.bfloat16):
    array = scale * jax.random.normal(stream_key, extent, jnp.float32)
    if split:
        array = array * shard_levels(stream_key, extent, split, -0.22, 0.18)
    return jnp.clip(raised(array, jax.random.fold_in(stream_key, 3), *heavy), -reach, reach).astype(kind)


def setup_inputs(seed: int = 0) -> dict:
    key_of = jax.random.split(jax.random.key(seed), 5)
    return {
        "blocks": noise_with(key_of[0], (NK, VIRT, NAUX), (NAUX ** -0.25), 0.75, ((0, 16), (2, 16)), (2, 1, 16, 2.0)),
        "vir_energy": jnp.clip(0.29882812 + 2.7011719 * jax.random.uniform(key_of[1], (NK, VIRT), jnp.float32) ** shard_levels(key_of[1], (NK, VIRT), ((0, 16),), -0.2, 0.2), 0.29882812, 3.0).astype(jnp.bfloat16),
        "occ_energy": jnp.clip(-1.0 + 0.80078125 * jax.random.uniform(key_of[2], (NK,), jnp.float32) ** shard_levels(key_of[2], (NK,), ((0, 16),), -0.2, 0.2), -1.0, -0.19921875).astype(jnp.bfloat16),
        "partner": jax.vmap(lambda own: jax.random.permutation(own, NK))(jax.random.split(key_of[3], NQ)).reshape((NQ, NK)).astype(jnp.int32),
    }


def pair_terms(own_block, mate_block, own_vir, mate_vir, own_occ, mate_occ):
    integral = lax.dot_general(own_block, mate_block, (((1,), (1,)), ((), ())), preferred_element_type=jnp.float32)
    denominator = (own_vir.astype(jnp.float32)[:, None] + mate_vir.astype(jnp.float32)[None, :]) - (own_occ.astype(jnp.float32) + mate_occ.astype(jnp.float32))
    direct = (integral / denominator).astype(jnp.bfloat16)
    paired = (2.0 * direct.astype(jnp.float32) - direct.T.astype(jnp.float32)).astype(jnp.bfloat16)
    own_term = jnp.dot(paired, mate_block, preferred_element_type=jnp.float32)
    partner_term = lax.dot_general(paired, own_block, (((0,), (0,)), ((), ())), preferred_element_type=jnp.float32)
    return own_term, partner_term.astype(jnp.bfloat16)


def reference(blocks, vir_energy, occ_energy, partner):
    def per_kpoint(kpoint):
        own_block = lax.dynamic_index_in_dim(blocks, kpoint, 0, keepdims=False)
        own_vir = lax.dynamic_index_in_dim(vir_energy, kpoint, 0, keepdims=False)
        own_occ = lax.dynamic_index_in_dim(occ_energy, kpoint, 0, keepdims=False)
        own_sum = jnp.zeros((VIRT, NAUX), jnp.float32)
        partner_terms = []
        for transfer in range(NQ):
            mate = lax.dynamic_index_in_dim(partner[transfer], kpoint, 0, keepdims=False).astype(jnp.int32)
            mate_block = lax.dynamic_index_in_dim(blocks, mate, 0, keepdims=False)
            mate_vir = lax.dynamic_index_in_dim(vir_energy, mate, 0, keepdims=False)
            mate_occ = lax.dynamic_index_in_dim(occ_energy, mate, 0, keepdims=False)
            own_term, partner_term = pair_terms(own_block, mate_block, own_vir, mate_vir, own_occ, mate_occ)
            own_sum = own_sum + own_term
            partner_terms.append(partner_term)
        return own_sum.astype(jnp.bfloat16), jnp.stack(partner_terms)

    gamma_own, stacked = lax.map(per_kpoint, jnp.arange(NK, dtype=jnp.int32))
    return gamma_own, jnp.transpose(stacked, (1, 0, 2, 3))
```

```python
import functools

import jax
import jax.numpy as jnp
from jax import lax
from jax.experimental import pallas as pl
from jax.experimental.pallas import tpu as pltpu
from jax.sharding import PartitionSpec as P

MESH = pl.DeviceIdType.MESH
DMA = pltpu.SemaphoreType.DMA
BF = jnp.bfloat16
F32 = jnp.float32

NK = 16
VIRT = 768
COLS = 256
ROWS = 48
HALF = 384
COL_A = pl.ds(0, HALF)
COL_B = pl.ds(HALF, HALF)
N_MSG = 100


def nt_dot(left, right):
    return lax.dot_general(left, right, (((1,), (1,)), ((), ())), preferred_element_type=F32)


def kernel(
    part, own, energy, out_own, out_mate,
    mid, stage, mate, all_energy, own_vir, integral,
    a_send, a_recv, a_direct, a_relay, a_final, a_ysend, a_yrecv,
    b_send, b_recv, b_direct, b_relay, b_final, b_ysend, b_yrecv,
    direct, send_sems, recv_sems,
):
    k = lax.axis_index("kring")
    c = lax.axis_index("cuts")
    z = c // 2
    h = lax.rem(c, 2)
    g = 1 - h

    def zpos(step):
        return lax.rem(z + step + 8, 8)

    def zdev(step):
        return (k, zpos(step) * 2 + h)

    ydev = (k, z * 2 + g)
    ring = [lax.rem(k + i, NK) for i in range(1, NK)]

    copies = []

    def send(src, dst, dev):
        copy = pltpu.make_async_remote_copy(
            src_ref=src,
            dst_ref=dst,
            send_sem=send_sems.at[len(copies)],
            recv_sem=recv_sems.at[len(copies)],
            device_id=dev,
            device_id_type=MESH,
        )
        copy.start()
        copies.append(copy)
        return copy

    barrier = pltpu.get_barrier_semaphore()
    peers = [(j, c) for j in ring] + [zdev(s) for s in (1, -1, 2, -2)] + [ydev]
    for dev in peers:
        pl.semaphore_signal(barrier, inc=1, device_id=dev, device_id_type=MESH)
    pl.semaphore_wait(barrier, len(peers))

    def piece(j):
        return pl.ds(pl.multiple_of(j * ROWS, ROWS), ROWS)

    first = [send(own.at[piece(j)], mid.at[k], (j, c)) for j in ring]
    mid[pl.ds(k, 1)] = own[piece(k)][None]
    all_energy[pl.ds(k, 1)] = energy[...][None]
    own_row = jnp.concatenate([energy[i : i + 1] for i in range(6)], axis=1)
    own_vir[...] = jnp.broadcast_to(own_row, (128, VIRT)).T
    for copy in first:
        copy.wait_recv()
    second = []
    for j in ring:
        stage[pl.ds(j, 1)] = mid[pl.ds(part[j], 1)]
        second.append(send(stage.at[j], mate.at[piece(k)], (j, c)))
    mate[piece(k)] = mid[part[k]]
    third = [send(energy, all_energy.at[k], (j, c)) for j in ring]
    for copy in second:
        copy.wait_recv()

    other = pl.ds(pl.multiple_of(g * HALF, HALF), HALF)
    mine = pl.ds(pl.multiple_of(h * HALF, HALF), HALF)
    b_ysend[...] = nt_dot(own[other], mate[COL_B]).astype(BF).reshape(8, ROWS, HALF)
    b_y = send(b_ysend, b_yrecv, ydev)
    for r in range(2):
        integral[r, :, :, COL_A] = nt_dot(own[pl.ds(r * HALF, HALF)], mate[COL_A]).reshape(8, ROWS, HALF)

    def reduce_start(chunk, out_buf, recv_buf, direct_buf, sign):
        plan = ((-3, -1, recv_buf.at[0]), (-4, -2, recv_buf.at[1]), (3, 1, recv_buf.at[2]),
                (-1, -1, direct_buf.at[0]), (1, 1, direct_buf.at[1]))
        sent = []
        for i, (dest, hop, target) in enumerate(plan):
            out_buf[i] = chunk(zpos(sign * dest)).astype(BF)
            sent.append(send(out_buf.at[i], target, zdev(sign * hop)))
        return sent

    def reduce_relay(chunk, sent, recv_buf, relay_buf, final_buf, sign):
        sent[0].wait_recv()
        sent[1].wait_recv()
        relay_buf[0] = (chunk(zpos(-2 * sign)) + recv_buf[0].astype(F32) + recv_buf[1].astype(F32)).astype(BF)
        near = send(relay_buf.at[0], final_buf.at[0], zdev(-2 * sign))
        sent[2].wait_recv()
        relay_buf[1] = (chunk(zpos(2 * sign)) + recv_buf[2].astype(F32)).astype(BF)
        far = send(relay_buf.at[1], final_buf.at[1], zdev(2 * sign))
        return [near, far]

    def reduce_end(chunk, sent, relayed, direct_buf, final_buf):
        for copy in sent[3:] + relayed:
            copy.wait_recv()
        return (chunk(z) + (direct_buf[0].astype(F32) + direct_buf[1].astype(F32))) + (
            final_buf[0].astype(F32) + final_buf[1].astype(F32)
        )

    def chunk_a(t):
        return integral[:, t, :, COL_A]

    def chunk_b(t):
        return integral[h, t, :, COL_B]

    a_sent = reduce_start(chunk_a, a_send, a_recv, a_direct, 1)
    integral[h, :, :, COL_B] = nt_dot(own[mine], mate[COL_B]).reshape(8, ROWS, HALF)
    b_y.wait_recv()
    integral[h, :, :, COL_B] += b_yrecv[...].astype(F32)
    b_sent = reduce_start(chunk_b, b_send, b_recv, b_direct, -1)
    a_relayed = reduce_relay(chunk_a, a_sent, a_recv, a_relay, a_final, 1)
    b_relayed = reduce_relay(chunk_b, b_sent, b_recv, b_relay, b_final, -1)

    for copy in third:
        copy.wait_recv()
    mate_energy = all_energy[part[k]]
    mate_row = jnp.concatenate([mate_energy[i : i + 1] for i in range(6)], axis=1)
    occupied = energy[6:7, 0:1] + mate_energy[6:7, 0:1]
    slot = h * 8 + z
    own_column = own_vir[piece(slot), 0:1]

    def amplitudes(total, cols):
        return (total / ((own_column + mate_row[:, cols]) - occupied)).astype(BF)

    total = reduce_end(chunk_a, a_sent, a_relayed, a_direct, a_final)
    integral[:, z, :, COL_A] = total
    a_ysend[...] = integral[g, z, :, COL_A].astype(BF)
    a_y = send(a_ysend, a_yrecv, ydev)

    def spread(at, cols, dev):
        view = direct.at[at, :, cols]
        return send(view, view, dev)

    def gather_start(at, cols):
        return [spread(at(0), cols, zdev(s)) for s in (1, -1, 2, -2)]

    def gather_relay(at, cols, sent, sign):
        sent[2 if sign > 0 else 3].wait_recv()
        on = [spread(at(-2 * sign), cols, zdev(sign * s)) for s in (2, 1)]
        sent[3 if sign > 0 else 2].wait_recv()
        back = [spread(at(2 * sign), cols, zdev(-sign))]
        return on + back

    def at_mine(step):
        return h * 8 + zpos(step)

    def at_other(step):
        return g * 8 + zpos(step)

    total = reduce_end(chunk_b, b_sent, b_relayed, b_direct, b_final)
    direct[slot, :, COL_B] = amplitudes(total, slice(HALF, VIRT))
    b_out = gather_start(at_mine, COL_B)
    b_cross = [spread(slot, COL_B, ydev)]

    a_y.wait_recv()
    total = integral[h, z, :, COL_A] + a_yrecv[...].astype(F32)
    direct[slot, :, COL_A] = amplitudes(total, slice(0, HALF))
    a_cross = spread(slot, COL_A, ydev)
    a_out = gather_start(at_mine, COL_A)

    b_on = gather_relay(at_mine, COL_B, b_out, -1)
    b_cross += [spread(at_mine(s), COL_B, ydev) for s in (2, -2)]
    for copy, s in ((b_out[0], -1), (b_out[1], 1)):
        copy.wait_recv()
        b_cross.append(spread(at_mine(s), COL_B, ydev))
    a_cross.wait_recv()
    a_other = gather_start(at_other, COL_A)
    a_on = gather_relay(at_mine, COL_A, a_out, 1)
    for copy, s in ((b_on[2], -3), (b_on[1], 3), (b_on[0], 4)):
        copy.wait_recv()
        b_cross.append(spread(at_mine(s), COL_B, ydev))
    a_other_on = gather_relay(at_other, COL_A, a_other, 1)
    for copy in a_out[:2] + a_on + a_other[:2] + a_other_on + b_cross:
        copy.wait_recv()

    amp = direct[...].reshape(VIRT, VIRT).astype(F32)
    flip = amp.T
    paired = (2.0 * amp - flip).astype(BF)
    out_own[...] = jnp.dot(paired, mate[...], preferred_element_type=F32).astype(BF)
    turned = (2.0 * flip - amp).astype(BF)
    out_mate[...] = jnp.dot(turned, own[...], preferred_element_type=F32).astype(BF)
    for copy in copies:
        copy.wait_send()


def on_device(blocks, vir_energy, occ_energy, partner):
    vir = vir_energy.astype(F32).reshape(6, 128)
    occ = jnp.broadcast_to(occ_energy.astype(F32).reshape(1, 1), (2, 128))
    energy = jnp.concatenate([vir, occ], axis=0)
    vmem = pl.BlockSpec(memory_space=pltpu.VMEM)
    chunk = (2, ROWS, HALF)
    half = (ROWS, HALF)
    gamma_own, gamma_mate = pl.pallas_call(
        kernel,
        out_shape=[jax.ShapeDtypeStruct((VIRT, COLS), BF)] * 2,
        in_specs=[pl.BlockSpec(memory_space=pltpu.SMEM), vmem, vmem],
        out_specs=[vmem, vmem],
        scratch_shapes=[
            pltpu.VMEM((NK, ROWS, COLS), BF),
            pltpu.VMEM((NK, ROWS, COLS), BF),
            pltpu.VMEM((VIRT, COLS), BF),
            pltpu.VMEM((NK, 8, 128), F32),
            pltpu.VMEM((VIRT, 128), F32),
            pltpu.VMEM((2, 8, ROWS, VIRT), F32),
            pltpu.VMEM((5,) + chunk, BF),
            pltpu.VMEM((3,) + chunk, BF),
            pltpu.VMEM((2,) + chunk, BF),
            pltpu.VMEM((2,) + chunk, BF),
            pltpu.VMEM((2,) + chunk, BF),
            pltpu.VMEM(half, BF),
            pltpu.VMEM(half, BF),
            pltpu.VMEM((5,) + half, BF),
            pltpu.VMEM((3,) + half, BF),
            pltpu.VMEM((2,) + half, BF),
            pltpu.VMEM((2,) + half, BF),
            pltpu.VMEM((2,) + half, BF),
            pltpu.VMEM((8,) + half, BF),
            pltpu.VMEM((8,) + half, BF),
            pltpu.VMEM((NK, ROWS, VIRT), BF),
            DMA((N_MSG,)),
            DMA((N_MSG,)),
        ],
        compiler_params=pltpu.CompilerParams(
            collective_id=0, has_side_effects=True, vmem_limit_bytes=56 * 1024 * 1024
        ),
        name="pair_window",
    )(partner.reshape(NK), blocks[0], energy)
    return gamma_own[None], gamma_mate[None, None]


def solution(mesh):
    return jax.shard_map(
        on_device,
        mesh=mesh,
        in_specs=(P("kring", None, "cuts"), P("kring", None), P("kring"), P()),
        out_specs=(P("kring", None, "cuts"), P(None, "kring", None, "cuts")),
        check_vma=False,
    )
```

```python
import jax
import jax.numpy as jnp
from jax import lax
from jax.experimental import pallas as pl
from jax.experimental.pallas import tpu as pltpu
from jax.sharding import PartitionSpec as P

MESH = pl.DeviceIdType.MESH
DMA = pltpu.SemaphoreType.DMA
BF = jnp.bfloat16
F32 = jnp.float32

NK = 16
VIRT = 768
COLS = 256
ROWS = 48
BAND = 96
HALF = 384
FAR_FIRST = (6, 2, 5, 3, 7, 1, 4, 0)
N_MSG = 100


def nt_dot(left, right):
    return lax.dot_general(left, right, (((1,), (1,)), ((), ())), preferred_element_type=F32)


def rows_at(index, size):
    return pl.ds(pl.multiple_of(index * size, size), size)


def kernel(
    part, own, energy, out_own, out_mate,
    mid, stage, own_pair, mate_pair, mate, all_energy, mate_energy, own_vir, denominator,
    integral, r_send, r_recv, r_direct, r_relay, r_final, away, amp,
    send_sems, recv_sems, mate_sems,
):
    k = lax.axis_index("kring")
    c = lax.axis_index("cuts")
    z = c // 2
    h = lax.rem(c, 2)
    g = 1 - h
    pair = k // 2
    q = lax.rem(k, 2)
    r = 1 - q
    work = 2 * pair + h
    sign = 1 - 2 * q

    def zpos(step):
        return lax.rem(z + step + 8, 8)

    def device(core, step, plane):
        return (2 * pair + core, 2 * zpos(step) + plane)

    other_core = (2 * pair + r, c)
    ids = {}

    def describe(name, src, dst, dev):
        at = ids.setdefault(name, len(ids))
        return pltpu.make_async_remote_copy(
            src_ref=src, dst_ref=dst, send_sem=send_sems.at[at], recv_sem=recv_sems.at[at],
            device_id=dev, device_id_type=MESH,
        )

    def send(name, src, dst, dev):
        copy = describe(name, src, dst, dev)
        copy.start()
        return copy

    def arrived(name, ref):
        describe(name, ref, ref, other_core).wait_recv()

    def left(name, ref):
        describe(name, ref, ref, other_core).wait_send()

    barrier = pltpu.get_barrier_semaphore()
    kring = [(2 * lax.rem(pair + i, 8) + core, i, core) for i in FAR_FIRST for core in (q, r)][:-2] + [
        (2 * pair + r, 0, r)
    ]
    peers = [(j, c) for j, _, _ in kring]
    peers += [(2 * lax.rem(pair + i, 8) + q, 2 * z + g) for i in range(8)] + [device(r, 0, g)]
    peers += [device(core, s, h) for core in (q, r) for s in (1, -1, 2, -2)]
    for dev in peers:
        pl.semaphore_signal(barrier, inc=1, device_id=dev, device_id_type=MESH)
    pl.semaphore_wait(barrier, len(peers))

    sent = []
    for n, (j, _, core) in enumerate(kring):
        sent.append(send(f"spread{n}", own.at[rows_at(core * 8 + j // 2, ROWS)], mid.at[k], (j, c)))

    mine_half = rows_at(q, HALF)

    @pl.when(q == h)
    def _():
        send("own_core", own, own_pair.at[h], other_core)

    @pl.when(q != h)
    def _():
        for core in (0, 1):
            half = pl.ds(core * HALF, HALF)
            send(f"own_y{core}", own.at[half], own_pair.at[h, half], device(core, 0, g))

    @pl.when(q == h)
    def _():
        own_pair[pl.ds(h, 1)] = own[...][None]

    mid[pl.ds(k, 1)] = own[rows_at(q * 8 + pair, ROWS)][None]
    all_energy[pl.ds(k, 1)] = energy[...][None]
    for n in range(15):
        arrived(f"spread{n}", mid.at[0])
    n = 0
    for i in FAR_FIRST:
        for plane in (g, h):
            target = lax.rem(pair + i, 8)
            wanted = mid[pl.ds(part[2 * target + plane], 1)]
            if i == 0 and plane is h:
                mate_pair[pl.ds(h, 1), rows_at(pair, ROWS)] = wanted
                continue
            stage[n] = wanted[0]
            sent.append(
                send(f"pick{n}", stage.at[n], mate_pair.at[h, rows_at(pair, ROWS)], (2 * target + q, 2 * z + plane))
            )
            n += 1

    def own_y_arrived():
        ref = own_pair.at[g, mine_half]
        at0 = ids["own_y0"]
        pltpu.make_async_remote_copy(
            src_ref=ref, dst_ref=ref, send_sem=send_sems.at[at0], recv_sem=recv_sems.at[at0 + q],
            device_id=other_core, device_id_type=MESH,
        ).wait_recv()

    own_y_arrived()
    sent.append(send("own_swap", own_pair.at[g, mine_half], own_pair.at[g, mine_half], other_core))
    for n, (j, _, _) in enumerate(kring):
        sent.append(send(f"energy{n}", energy, all_energy.at[k], (j, c)))

    @pl.when(q != h)
    def _():
        arrived("own_core", own)

    for n in range(15):
        arrived(f"pick{n}", stage.at[0])
    arrived("own_swap", own_pair.at[g, mine_half])

    for b in range(4):
        band = pl.ds(b * 192, 192)
        integral[pl.ds(2 * b, 2)] = (
            nt_dot(own_pair[0, band], mate_pair[0]) + nt_dot(own_pair[1, band], mate_pair[1])
        ).reshape(2, BAND, HALF)

    plan = ((-4, -2, r_recv.at[1]), (-3, -1, r_recv.at[0]), (3, 1, r_recv.at[2]),
            (-1, -1, r_direct.at[0]), (1, 1, r_direct.at[1]))
    starts = []
    for i, (dest, hop, target) in enumerate(plan):
        r_send[i] = integral[zpos(sign * dest)].astype(BF)
        starts.append(send(f"part{i}", r_send.at[i], target, device(q, sign * hop, h)))
    sent += starts

    def mate_copy(dst_core, plane, src):
        return pltpu.make_async_remote_copy(
            src_ref=src, dst_ref=mate.at[mine_half], send_sem=mate_sems.at[2], recv_sem=mate_sems.at[q],
            device_id=device(dst_core, 0, plane), device_id_type=MESH,
        )

    mate_copy(h, g, mate_pair.at[g]).start()

    @pl.when(q == h)
    def _():
        mate[mine_half] = mate_pair[h]

    @pl.when(q != h)
    def _():
        send("mate_core", mate_pair.at[h], mate.at[mine_half], other_core)

    for n in range(15):
        arrived(f"energy{n}", energy)
    mate_energy[...] = all_energy[part[work]]
    work_energy = all_energy[work]
    own_row = jnp.concatenate([work_energy[i : i + 1] for i in range(6)], axis=1)
    own_vir[...] = jnp.broadcast_to(own_row, (128, VIRT)).T
    mate_row = jnp.concatenate([mate_energy[pl.ds(q * 3 + i, 1)] for i in range(3)], axis=1)
    occupied = work_energy[6:7, 0:1] + mate_energy[6:7, 0:1]
    denominator[...] = (own_vir[rows_at(z, BAND), 0:1] + mate_row) - occupied

    starts[0].wait_recv()
    starts[1].wait_recv()
    r_relay[0] = (integral[zpos(-2 * sign)] + r_recv[0].astype(F32) + r_recv[1].astype(F32)).astype(BF)
    sent.append(send("relay0", r_relay.at[0], r_final.at[0], device(q, -2 * sign, h)))
    starts[2].wait_recv()
    r_relay[1] = (integral[zpos(2 * sign)] + r_recv[2].astype(F32)).astype(BF)
    sent.append(send("relay1", r_relay.at[1], r_final.at[1], device(q, 2 * sign, h)))
    starts[3].wait_recv()
    starts[4].wait_recv()
    total = integral[z] + (r_direct[0].astype(F32) + r_direct[1].astype(F32))
    for n in range(2):
        arrived(f"relay{n}", r_final.at[0])
    total = total + (r_final[0].astype(F32) + r_final[1].astype(F32))
    chunk = (total / denominator[...]).astype(BF)

    block = amp.at[0, 0]
    near = (2, -2, 1, -1)

    def pass_on(tag, half, way):
        arrived(f"{tag}first{2 * way}", block)
        out = [
            send(f"{tag}on{s}", amp.at[half, zpos(-2 * way)], amp.at[half, zpos(-2 * way)], device(q, s * way, h))
            for s in (2, 1)
        ]
        arrived(f"{tag}first{-2 * way}", block)
        view = amp.at[half, zpos(2 * way)]
        out.append(send(f"{tag}back", view, view, device(q, -way, h)))
        return out

    def late(tag, way):
        return ((f"{tag}on2", -4 * way), (f"{tag}on1", -3 * way), (f"{tag}back", 3 * way))

    @pl.when(q == h)
    def _():
        amp[q, z] = chunk
        view = amp.at[q, z]
        out = [send(f"b_first{s}", view, view, device(q, s, h)) for s in near]

        def cross(step):
            view = amp.at[q, zpos(step)]
            out.append(send(f"cross{step}", view, view, device(q, 0, g)))

        cross(0)
        out.extend(pass_on("b_", q, 1))
        cross(-2)
        cross(2)
        out.extend(pass_on("a_", r, -1))
        for s in (1, -1):
            arrived(f"b_first{s}", block)
            cross(-s)
        for name, step in late("b_", 1):
            arrived(name, block)
            cross(step if step > -4 else 4)
        arrived("a_own", block)
        for s in (1, -1):
            arrived(f"a_first{s}", block)
        for name, _ in late("a_", -1):
            arrived(name, block)
        arrived("mate_core", mate.at[mine_half])
        for copy in out:
            copy.wait_send()

    @pl.when(q != h)
    def _():
        away[...] = chunk
        target = amp.at[q, z]
        out = [send("a_y", away, target, device(r, 0, g))]
        out += [send(f"a_first{s}", away, target, device(r, s, h)) for s in near]
        out += [send("a_own", away, target, other_core)]
        arrived("a_y", block)
        view = amp.at[r, z]
        second = []
        for s in near:
            second.append(send(f"a_away{s}", view, view, device(q, s, h)))
        out += second
        for s in (2,):
            arrived(f"a_away{-s}", block)
            for t in (2, 1):
                v = amp.at[r, zpos(2)]
                out.append(send(f"a_on{t}", v, v, device(q, -t, h)))
            arrived(f"a_away{s}", block)
            v = amp.at[r, zpos(-2)]
            out.append(send("a_back", v, v, device(q, 1, h)))
        for s in (1, -1):
            arrived(f"a_away{s}", block)
        for step in (0, -2, 2, 1, -1, 4, -3, 3):
            arrived(f"cross{step}", block)
        for name, _ in late("a_", -1):
            arrived(name, block)
        for core in (0, 1):
            pltpu.make_async_remote_copy(
                src_ref=mate.at[mine_half], dst_ref=mate.at[mine_half], send_sem=mate_sems.at[2],
                recv_sem=mate_sems.at[core], device_id=other_core, device_id_type=MESH,
            ).wait_recv()
        for copy in out:
            copy.wait_send()

    full = jnp.concatenate([amp[0].reshape(VIRT, HALF), amp[1].reshape(VIRT, HALF)], axis=1).astype(F32)
    flip = full.T
    paired = (2.0 * full - flip).astype(BF)
    out_own[...] = jnp.dot(paired, mate[...], preferred_element_type=F32).astype(BF)
    turned = (2.0 * flip - full).astype(BF)
    out_mate[...] = jnp.dot(turned, own[...], preferred_element_type=F32).astype(BF)

    for copy in sent:
        copy.wait_send()
    mate_copy(h, g, mate_pair.at[g]).wait_send()

    @pl.when(q == h)
    def _():
        left("own_core", own)

    @pl.when(q != h)
    def _():
        for core in (0, 1):
            left(f"own_y{core}", own.at[mine_half])
        left("mate_core", mate_pair.at[h])


def on_device(blocks, vir_energy, occ_energy, partner):
    vir = vir_energy.astype(F32).reshape(6, 128)
    occ = jnp.broadcast_to(occ_energy.astype(F32).reshape(1, 1), (2, 128))
    energy = jnp.concatenate([vir, occ], axis=0)
    vmem = pl.BlockSpec(memory_space=pltpu.VMEM)
    unit = (BAND, HALF)
    gamma_own, gamma_mate = pl.pallas_call(
        kernel,
        out_shape=[jax.ShapeDtypeStruct((VIRT, COLS), BF)] * 2,
        in_specs=[pl.BlockSpec(memory_space=pltpu.SMEM), vmem, vmem],
        out_specs=[vmem, vmem],
        scratch_shapes=[
            pltpu.VMEM((NK, ROWS, COLS), BF),
            pltpu.VMEM((NK, ROWS, COLS), BF),
            pltpu.VMEM((2, VIRT, COLS), BF),
            pltpu.VMEM((2, HALF, COLS), BF),
            pltpu.VMEM((VIRT, COLS), BF),
            pltpu.VMEM((NK, 8, 128), F32),
            pltpu.VMEM((8, 128), F32),
            pltpu.VMEM((VIRT, 128), F32),
            pltpu.VMEM(unit, F32),
            pltpu.VMEM((8,) + unit, F32),
            pltpu.VMEM((5,) + unit, BF),
            pltpu.VMEM((3,) + unit, BF),
            pltpu.VMEM((2,) + unit, BF),
            pltpu.VMEM((2,) + unit, BF),
            pltpu.VMEM((2,) + unit, BF),
            pltpu.VMEM(unit, BF),
            pltpu.VMEM((2, 8) + unit, BF),
            DMA((N_MSG,)),
            DMA((N_MSG,)),
            DMA((3,)),
        ],
        compiler_params=pltpu.CompilerParams(
            collective_id=0, has_side_effects=True, vmem_limit_bytes=24 * 1024 * 1024
        ),
        name="pair_window",
    )(partner.reshape(NK), blocks[0], energy)
    return gamma_own[None], gamma_mate[None, None]


def solution(mesh):
    return jax.shard_map(
        on_device,
        mesh=mesh,
        in_specs=(P("kring", None, "cuts"), P("kring", None), P("kring"), P()),
        out_specs=(P("kring", None, "cuts"), P(None, "kring", None, "cuts")),
        check_vma=False,
    )
```
